32 devices in a mesh: lon: 16 (over z, x, core), lat: 2 (over y).
Axes of the slice: x: 2, y: 2, z: 4, core: 2. Of those that a mesh axis runs over, the one named last changes fastest.
Arguments:
- spec_pts: bfloat16 [36, 36, 16384], P(None, None, ('lon', 'lat')), may hold values from 0.049804688 to 2
- wind_u: float32 [16384], P(('lon', 'lat')), may hold values from -40 to 40
- wind_v: float32 [16384], P(('lon', 'lat')), may hold values from -40 to 40
- ocean_current: bfloat16 [2, 2, 128, 128], P(None, 'lat', 'lon'), may hold values from -0.099609375 to 0.099609375
- block_owner: int32 [8, 16], P('lat', 'lon'), may hold values from 0 to 15, as said below
- block_slot: int32 [8, 16], P('lat', 'lon'), may hold values from 0 to 7, as said below
- cell_source: int32 [8, 2048], P('lat', 'lon'), may hold values from 0 to 511, as said below
- land_mask: int32 [8, 2048], P('lat', 'lon'), may hold values 0 or 1
Outputs:
- spectrum_out: bfloat16 [36, 36, 8, 2048], P(None, None, 'lat', 'lon')
The draws below stay inside these ranges and needn't reach their ends.
Inputs may be any that keep to these rules, and one draw needn't show every extreme that they name: Within each band of 4 grid rows, the pairs (block_owner, block_slot) over all its rows and tile columns are distinct, each owner's slots run from 0 to its count of blocks minus one; an owner holds between 0 and 8 blocks, and at least one owner holds exactly 8. `block_slot`: see block_owner. `cell_source`: within each tile of 4 x 128 cells, the values are a permutation of 0 to 511.
All inputs are finite; a program needn't handle non-finite values. No bound on the sum of `land_mask` on one device may be relied on, other than what follows from the above.
Results may differ from the reference program's by a relative error of at most 0.001.
The reference program's roundings to bfloat16 on the way count: a program that leaves them out, or rounds other values in their place, can miss the bound.
Values may be sent and summed in bfloat16 or wider, within the bound.
No kernel may reach another device: no remote copies, remote signals or barrier semaphores. Data moves between devices by JAX's collectives and lax.ppermute only.
A program may use at most 128 MiB of HBM per device.

```python
import math
import jax
import jax.numpy as jnp
from jax import lax

NF = 36
ND = 36
LATC = 4
LONC = 128
TILE = 512
SLOTS = 16
CAP = 8
NY = 8
NX = 2048
PTS = 16384
N_LON = 16
N_LAT = 2


def owner_layout(key):

    def group(index):
        sub = jax.random.fold_in(key, index)
        first_key, second_key, third_key = jax.random.split(sub, 3)
        half = N_LON // 2
        extra = jax.random.randint(first_key, (half,), 0, LATC + 1)
        extra = extra.at[0].set(LATC)
        counts = jnp.stack([LATC + extra, LATC - extra], axis=1).reshape(-1)
        counts = counts[jax.random.permutation(second_key, N_LON)]
        ends = jnp.cumsum(counts)
        starts = ends - counts
        blocks = jnp.arange(LATC * N_LON).astype(jnp.int32)
        owner = jnp.searchsorted(ends, blocks, side='right').astype(jnp.int32)
        slot = (blocks - starts[owner]).astype(jnp.int32)
        shuffle = jax.random.permutation(third_key, LATC * N_LON)
        return (owner[shuffle].reshape(LATC, N_LON), slot[shuffle].reshape(LATC, N_LON))
    owners, slots = jax.vmap(group)(jnp.arange(N_LAT).astype(jnp.int32))
    return (owners.reshape(N_LAT * LATC, N_LON), slots.reshape(N_LAT * LATC, N_LON))


def draw_block_owner(key, part):
    return owner_layout(jax.random.fold_in(key, 7))[0]


def draw_block_slot(key, part):
    return owner_layout(jax.random.fold_in(key, 7))[1]


def draw_cell_source(key, part):
    base = jax.random.fold_in(key, 13)
    tiles = jnp.arange(N_LAT * N_LON).astype(jnp.int32)
    perms = jax.vmap(lambda index: jax.random.permutation(jax.random.fold_in(base, index), TILE))(tiles)
    perms = perms.reshape(N_LAT, N_LON, LATC, LONC).transpose(0, 2, 1, 3)
    return perms.reshape(N_LAT * LATC, N_LON * LONC).astype(jnp.int32)


def place_ends(drawn, stream_key, low, top_value):
    shape = drawn.shape
    spot = [jax.random.randint(jax.random.fold_in(stream_key, axis), (), 0, shape[axis]) for axis in range(len(shape))]
    drawn = drawn.at[tuple(spot)].set(low)
    longest = shape.index(max(shape))
    spot[longest] = (spot[longest] + 1) % shape[longest]
    return drawn.at[tuple(spot)].set(top_value)


def block_scale(rng, extent, cuts, least, largest):
    level, own = 1.0, jax.random.fold_in(rng, 6)
    for position, parts in cuts:
        draws = jnp.exp(jax.random.uniform(jax.random.fold_in(own, position), (parts,), jnp.float32, least / len(cuts), largest / len(cuts)))
        level = level * jnp.repeat(draws, extent[position] // parts).reshape([-1 if axis == position else 1 for axis in range(len(extent))])
    return level


def centred(rng, extent, scale, bound, cuts=(), held_as=jnp.bfloat16):
    drawn = jax.random.normal(rng, extent, jnp.float32) * scale
    if len(cuts) > 0:
        drawn = block_scale(rng, extent, cuts, -0.22, 0.18) * drawn
    return jnp.clip(drawn, min=-bound, max=bound).astype(held_as)


def setup_inputs(seed: int = 0) -> dict:
    splits = jax.random.split(jax.random.key(seed), 9)
    return {
        "spec_pts": jnp.clip(jnp.exp(math.log(2.0) - 3.6927934 * jax.random.uniform(splits[0], (NF, ND, PTS), jnp.float32) ** block_scale(splits[0], (NF, ND, PTS), ((2, 32),), -0.2, 0.2)), 0.049804688, 2.0).astype(jnp.bfloat16),
        "wind_u": centred(splits[1], (PTS,), 8.0, 40.0, ((0, 32),), jnp.float32),
        "wind_v": centred(splits[2], (PTS,), 8.0, 40.0, ((0, 32),), jnp.float32),
        "ocean_current": jnp.clip(jax.random.uniform(splits[3], (2, N_LAT, N_LON * CAP, LONC), jnp.float32, -0.099609375, 0.099609375) * block_scale(splits[3], (2, N_LAT, N_LON * CAP, LONC), ((1, 2), (2, 16)), -0.4, 0.0), -0.099609375, 0.099609375).astype(jnp.bfloat16),
        "block_owner": draw_block_owner(jax.random.fold_in(splits[8], 71), 0),
        "block_slot": draw_block_slot(jax.random.fold_in(splits[8], 71), 0),
        "cell_source": draw_cell_source(jax.random.fold_in(splits[8], 71), 0),
        "land_mask": place_ends((jax.random.randint(splits[7], (NY, NX), 0, 5) < 4).astype(jnp.int32), jax.random.fold_in(splits[7], 1), 0, 1),
    }


fastest = 0.53
turn_scale = 2.5


def tables(freqs, dirs):
    ratio = 1.1 ** jnp.arange(freqs).astype(jnp.float32)
    group_speed = fastest / ratio
    phase_speed = 44.6 / ratio
    relative = ratio / ratio[freqs - 1]
    spacing = 2.0 * jnp.pi / dirs
    theta = (jnp.arange(dirs).astype(jnp.float32) + 0.5) * spacing
    facing = (jnp.arange(dirs).astype(jnp.float32) + 1.0) * spacing
    return group_speed, phase_speed, relative, jnp.cos(theta), jnp.sin(theta), jnp.cos(facing), jnp.sin(facing)


def grow(energy, proj, phase_val, rel_val, mean_energy):
    drive = jnp.maximum(proj / phase_val - 1.0, 0.0)
    gain = 0.5 * jnp.tanh(0.2 * drive)
    loss = 0.3 * rel_val * (mean_energy / 0.5) ** 2
    return (energy * jnp.exp(gain - loss)).astype(jnp.bfloat16)


def turning(ux, uy, vx, vy, face_cos, face_sin):
    return turn_scale * (face_sin * face_cos * (ux - vy) + face_sin * face_sin * uy - face_cos * face_cos * vx)


def refract(moved, turn):
    upper = jnp.roll(moved, -1, axis=0)
    flux = jnp.maximum(turn, 0.0) * moved + jnp.minimum(turn, 0.0) * upper
    return moved - (flux - jnp.roll(flux, 1, axis=0))


def reference(spec_pts, wind_u, wind_v, ocean_current, block_owner, block_slot, cell_source, land_mask):
    group_speed, phase_speed, relative, cosd, sind, face_cos, face_sin = tables(NF, ND)
    mean_energy = jnp.sum(spec_pts.astype(jnp.float32), axis=(0, 1)) / (NF * ND)
    proj = wind_u[None, :] * cosd[:, None] + wind_v[None, :] * sind[:, None]
    rows = jnp.arange(NY).astype(jnp.int32)[:, None]
    cols = jnp.arange(NX).astype(jnp.int32)[None, :]
    tile_flat = (rows // LATC) * N_LON + cols // LONC
    slot_rest = cell_source % SLOTS
    source = cell_source // SLOTS
    point = ((source % N_LON) * N_LAT + source // N_LON) * TILE + tile_flat * SLOTS + slot_rest
    index = block_owner * CAP + block_slot
    band = (jnp.arange(NY).astype(jnp.int32) // LATC)[:, None]
    current = ocean_current[:, band, index, :].reshape(2, NY, NX).astype(jnp.float32)
    east_u, east_v = current[0], current[1]
    sea = land_mask.astype(jnp.float32)
    zero_row = jnp.zeros((1, NX), jnp.float32)
    north = lambda a: jnp.concatenate([a[1:], zero_row], axis=0)
    south = lambda a: jnp.concatenate([zero_row, a[:-1]], axis=0)
    open_x = sea * jnp.roll(sea, -1, axis=1)
    face_u = 0.5 * (east_u + jnp.roll(east_u, -1, axis=1))
    open_y = sea * north(sea)
    face_v = 0.5 * (east_v + north(east_v))
    ux = 0.5 * (jnp.roll(east_u, -1, axis=1) - jnp.roll(east_u, 1, axis=1))
    vx = 0.5 * (jnp.roll(east_v, -1, axis=1) - jnp.roll(east_v, 1, axis=1))
    uy = 0.5 * (north(east_u) - south(east_u))
    vy = 0.5 * (north(east_v) - south(east_v))
    turn = turning(ux[None], uy[None], vx[None], vy[None], face_cos[:, None, None], face_sin[:, None, None])

    def one_freq(freq):
        sourced = grow(spec_pts[freq].astype(jnp.float32), proj, phase_speed[freq], relative[freq], mean_energy[None, :])
        energy = (sourced[:, point] * land_mask.astype(jnp.bfloat16)[None]).astype(jnp.float32)
        cx = group_speed[freq] * cosd[:, None, None] + face_u[None]
        flux_x = open_x[None] * (jnp.maximum(cx, 0.0) * energy + jnp.minimum(cx, 0.0) * jnp.roll(energy, -1, axis=2))
        div_x = flux_x - jnp.roll(flux_x, 1, axis=2)
        energy_n = jnp.concatenate([energy[:, 1:], jnp.zeros((ND, 1, NX), jnp.float32)], axis=1)
        cy = group_speed[freq] * sind[:, None, None] + face_v[None]
        flux_y = open_y[None] * (jnp.maximum(cy, 0.0) * energy + jnp.minimum(cy, 0.0) * energy_n)
        div_y = flux_y - jnp.concatenate([jnp.zeros((ND, 1, NX), jnp.float32), flux_y[:, :-1]], axis=1)
        moved = energy - div_x - div_y
        return (refract(moved, turn) * sea[None]).astype(jnp.bfloat16)

    return lax.map(one_freq, jnp.arange(NF).astype(jnp.int32))
```

```python
import functools

import jax
import jax.numpy as jnp
import numpy as np
from jax import lax
from jax.experimental import pallas as pl
from jax.experimental.pallas import tpu as pltpu
from jax.sharding import PartitionSpec as P

fastest = 0.53
turn_scale = 2.5

VMEM = pl.BlockSpec(memory_space=pltpu.VMEM)
SMEM = pl.BlockSpec(memory_space=pltpu.SMEM)


def tables(freqs, dirs):
    ratio = 1.1 ** np.arange(freqs)
    spacing = 2.0 * np.pi / dirs
    theta = (np.arange(dirs) + 0.5) * spacing
    facing = (np.arange(dirs) + 1.0) * spacing
    f32 = np.float32
    return dict(
        group=(fastest / ratio).astype(f32),
        slow=(ratio / 44.6).astype(f32),
        rel=(ratio / ratio[freqs - 1]).astype(f32),
        cosd=np.cos(theta).astype(f32),
        sind=np.sin(theta).astype(f32),
        fcos=np.cos(facing).astype(f32),
        fsin=np.sin(facing).astype(f32),
    )


def source_kernel(slow_ref, rel_ref, spec_ref, u_ref, v_ref, trig_ref, out_ref):
    freqs, dirs, points = spec_ref.shape

    def add(f, acc):
        return acc + spec_ref[f].astype(jnp.float32)

    acc = lax.fori_loop(0, freqs, add, jnp.zeros((dirs, points), jnp.float32), unroll=4)
    mean = jnp.sum(acc, axis=0, keepdims=True) / (freqs * dirs)
    base = 0.3 * (mean / 0.5) ** 2
    proj = u_ref[...] * trig_ref[:, 0:1] + v_ref[...] * trig_ref[:, 1:2]

    def one(f, carry):
        drive = jnp.maximum(proj * slow_ref[f] - 1.0, 0.0)
        gain = 0.5 * jnp.tanh(0.2 * drive)
        grown = spec_ref[f].astype(jnp.float32) * jnp.exp(gain - rel_ref[f] * base)
        out_ref[f] = grown.astype(jnp.bfloat16)
        return carry

    lax.fori_loop(0, freqs, one, 0, unroll=2)


def source(tab, spec, wind_u, wind_v):
    trig = np.stack([tab["cosd"], tab["sind"]], axis=1)
    return pl.pallas_call(
        source_kernel,
        out_shape=jax.ShapeDtypeStruct(spec.shape, jnp.bfloat16),
        in_specs=[SMEM, SMEM, VMEM, VMEM, VMEM, VMEM],
        out_specs=VMEM,
        name="source",
    )(tab["slow"], tab["rel"], spec, wind_u[None], wind_v[None], trig)


def regroup_kernel(recv_ref, cell_ref, mask_ref, want_ref, ocean_ref, tile_ref, rows_ref, cols_ref, aux_ref):
    points, spectral = recv_ref.shape
    lat_rows, lon_cells = cell_ref.shape
    cell = cell_ref[...]
    mask = mask_ref[...]
    index = lax.broadcasted_iota(jnp.int32, (points, lon_cells), 0)
    hots = [
        jnp.where((index == cell[y : y + 1]) & (mask[y : y + 1] > 0), 1.0, 0.0).astype(jnp.bfloat16)
        for y in range(lat_rows)
    ]
    hot = jnp.concatenate(hots, axis=1)
    recv = recv_ref[...]
    dims = (((0,), (0,)), ((), ()))
    tile = lax.dot_general(recv, hot, dims, preferred_element_type=jnp.float32).astype(jnp.bfloat16)
    tile_ref[...] = tile
    blocks = ocean_ref.shape[1]
    pick = (lax.broadcasted_iota(jnp.int32, (lat_rows, blocks), 1) == want_ref[...]).astype(jnp.bfloat16)
    u = jnp.dot(pick, ocean_ref[0], preferred_element_type=jnp.float32)
    v = jnp.dot(pick, ocean_ref[1], preferred_element_type=jnp.float32)
    sea = mask.astype(jnp.float32)
    aux_ref[0] = u
    aux_ref[1] = v
    aux_ref[2] = sea
    for i, y in enumerate((0, lat_rows - 1)):
        rows_ref[i, :spectral] = tile[:, y * lon_cells : (y + 1) * lon_cells]
        extra = jnp.concatenate(
            [u[y : y + 1], v[y : y + 1], sea[y : y + 1], jnp.zeros((5, lon_cells), jnp.float32)], axis=0
        )
        rows_ref[i, spectral:] = extra.astype(jnp.bfloat16)
    lanes = lax.broadcasted_iota(jnp.int32, (lat_rows, points), 1)
    pad = cols_ref.shape[2] - spectral
    spot = lax.broadcasted_iota(jnp.int32, (lat_rows, pad), 1)
    for i, x in enumerate((0, lon_cells - 1)):
        edge = jnp.where((lanes == cell[:, x : x + 1]) & (mask[:, x : x + 1] > 0), 1.0, 0.0).astype(jnp.bfloat16)
        values = jnp.dot(edge, recv, preferred_element_type=jnp.float32)
        extra = jnp.where(
            spot == 0, u[:, x : x + 1], jnp.where(spot == 1, v[:, x : x + 1], jnp.where(spot == 2, sea[:, x : x + 1], 0.0))
        )
        cols_ref[i] = jnp.concatenate([values, extra], axis=1).astype(jnp.bfloat16)


def regroup(recv, cell, mask, want, ocean):
    points, spectral = recv.shape
    lat_rows, lon_cells = cell.shape
    wide = -(-(spectral + 3) // 128) * 128
    return pl.pallas_call(
        regroup_kernel,
        out_shape=(
            jax.ShapeDtypeStruct((spectral, points), jnp.bfloat16),
            jax.ShapeDtypeStruct((2, spectral + 8, lon_cells), jnp.bfloat16),
            jax.ShapeDtypeStruct((2, lat_rows, wide), jnp.bfloat16),
            jax.ShapeDtypeStruct((3, lat_rows, lon_cells), jnp.float32),
        ),
        in_specs=[VMEM] * 5,
        out_specs=(VMEM,) * 4,
        name="regroup",
    )(recv, cell, mask, want, ocean)


def upwind(speed, here, there):
    return jnp.where(speed > 0.0, here, there) * speed


def step_kernel(group_ref, tile_ref, south_ref, north_ref, west_ref, east_ref, cols_ref, aux_ref, trig_ref, freq_ref, out_ref, halo, turns, lay):
    spectral = tile_ref.shape[0]
    rows, lanes = turns.shape[1], aux_ref.shape[2]
    lat_rows = aux_ref.shape[1]
    dirs = rows // 2
    f32 = jnp.float32
    u, v, sea = aux_ref[0], aux_ref[1], aux_ref[2]
    lane = lax.broadcasted_iota(jnp.int32, (lat_rows, lanes), 1)
    west = west_ref[...].astype(f32)
    east = east_ref[...].astype(f32)

    def sides(a, i):
        at = spectral + i
        right = jnp.where(lane == lanes - 1, east[:, at : at + 1], pltpu.roll(a, lanes - 1, 1))
        left = jnp.where(lane == 0, west[:, at : at + 1], pltpu.roll(a, 1, 1))
        return left, right

    uw, ue = sides(u, 0)
    vw, ve = sides(v, 1)
    _, me = sides(sea, 2)
    open_x = sea * me
    face_u = 0.5 * (u + ue)
    below = south_ref[spectral : spectral + 8].astype(f32)
    above = north_ref[spectral : spectral + 8].astype(f32)
    ut = jnp.concatenate([below[0:1], u, above[0:1]], axis=0)
    vt = jnp.concatenate([below[1:2], v, above[1:2]], axis=0)
    mt = jnp.concatenate([below[2:3], sea, above[2:3]], axis=0)
    open_y = mt[:-1] * mt[1:]
    face_v = 0.5 * (vt[:-1] + vt[1:])
    ux = 0.5 * (ue - uw)
    vx = 0.5 * (ve - vw)
    uy = 0.5 * (ut[2:] - ut[:-2])
    vy = 0.5 * (vt[2:] - vt[:-2])
    fc, fs = trig_ref[:, 2:3], trig_ref[:, 3:4]
    for y in range(lat_rows):
        sl = slice(y, y + 1)
        turns[y] = turn_scale * (fs * fc * (ux[sl] - vy[sl]) + fs * fs * uy[sl] - fc * fc * vx[sl])
    own = cols_ref[0, :, :spectral].astype(f32)
    wide_u = west[:, spectral : spectral + 1]
    speed = freq_ref[0:1] + 0.5 * (wide_u + u[:, 0:1])
    flux_w = (west[:, spectral + 2 : spectral + 3] * sea[:, 0:1]) * upwind(speed, west[:, :spectral], own)
    hi = flux_w.astype(jnp.bfloat16)
    rest = flux_w - hi.astype(f32)
    mid = rest.astype(jnp.bfloat16)
    low = (rest - mid.astype(f32)).astype(jnp.bfloat16)
    left = jnp.concatenate([hi, mid, low, east_ref[:, :spectral]], axis=0)
    total = lat_rows * lanes
    j = lax.broadcasted_iota(jnp.int32, (4 * lat_rows, total), 0)
    c = lax.broadcasted_iota(jnp.int32, (4 * lat_rows, total), 1)
    part, jy = j // lat_rows, j % lat_rows
    place = jnp.where(c == jy * lanes + jnp.where(part == 3, lanes - 1, 0), 1.0, 0.0).astype(jnp.bfloat16)
    halo[...] = lax.dot_general(left, place, (((0,), (0,)), ((), ())), preferred_element_type=f32)

    row = lax.broadcasted_iota(jnp.int32, (rows, lanes), 0)
    full_lane = lax.broadcasted_iota(jnp.int32, (rows, lanes), 1)
    is_last, is_first = full_lane == lanes - 1, full_lane == 0
    top = row < dirs
    seam_up = (row == dirs - 1) | (row == rows - 1)
    seam_down = (row == 0) | (row == dirs)
    cosd, sind = trig_ref[:, 0:1], trig_ref[:, 1:2]

    def pair(i, carry):
        at = pl.multiple_of(i * rows, 8)
        sl = pl.ds(at, rows)
        speed_f = jnp.where(top, group_ref[2 * i], group_ref[2 * i + 1])
        gc = speed_f * cosd
        gs = speed_f * sind
        value = [tile_ref[sl, y * lanes : (y + 1) * lanes].astype(f32) for y in range(lat_rows)]
        below_v = south_ref[sl, :].astype(f32)
        above_v = north_ref[sl, :].astype(f32)
        flux_s = None
        for y in range(lat_rows + 1):
            lower = below_v if y == 0 else value[y - 1]
            upper = above_v if y == lat_rows else value[y]
            cy = gs + face_v[y : y + 1]
            flux_n = open_y[y : y + 1] * upwind(cy, lower, upper)
            if y > 0:
                k = y - 1
                e = value[k]
                edge = halo[sl, k * lanes : (k + 1) * lanes]
                ee = jnp.where(is_last, edge, pltpu.roll(e, lanes - 1, 1))
                cx = gc + face_u[k : k + 1]
                fx = open_x[k : k + 1] * upwind(cx, e, ee)
                fw = jnp.where(is_first, edge, pltpu.roll(fx, 1, 1))
                moved = e - (fx - fw) - (flux_n - flux_s)
                up = jnp.where(seam_up, pltpu.roll(moved, dirs - 1, 0), pltpu.roll(moved, rows - 1, 0))
                g = upwind(turns[k], moved, up)
                gp = jnp.where(seam_down, pltpu.roll(g, dirs + 1, 0), pltpu.roll(g, 1, 0))
                lay[pl.ds(k, rows, stride=lat_rows), :] = (moved - (g - gp)) * sea[k : k + 1]
            flux_s = flux_n
        out_ref[pl.ds(pl.multiple_of(at * lat_rows, 8), rows * lat_rows), :] = lay[...].astype(jnp.bfloat16)
        return carry

    lax.fori_loop(0, spectral // rows, pair, 0)


def step(tab, tile, south, north, west, east, cols, aux):
    spectral, points = tile.shape
    freqs, dirs = tab["group"].shape[0], tab["cosd"].shape[0]
    _, lat_rows, lon_cells = aux.shape
    trig = np.tile(np.stack([tab["cosd"], tab["sind"], tab["fcos"], tab["fsin"]], axis=1), (2, 1))
    freq = np.outer(tab["group"], tab["cosd"]).reshape(1, spectral)
    return pl.pallas_call(
        step_kernel,
        out_shape=jax.ShapeDtypeStruct((spectral * lat_rows, lon_cells), jnp.bfloat16),
        in_specs=[SMEM] + [VMEM] * 9,
        out_specs=VMEM,
        scratch_shapes=[
            pltpu.VMEM((spectral, points), jnp.float32),
            pltpu.VMEM((lat_rows, 2 * dirs, lon_cells), jnp.float32),
            pltpu.VMEM((2 * dirs * lat_rows, lon_cells), jnp.float32),
        ],
        name="step",
    )(tab["group"], tile, south, north, west, east, cols, aux, trig, freq)


def body(spec_pts, wind_u, wind_v, ocean_current, block_owner, block_slot, cell_source, land_mask):
    freqs, dirs, points = spec_pts.shape
    lat_rows, lon_cells = cell_source.shape
    n_lon, n_lat = lax.axis_size("lon"), lax.axis_size("lat")
    per_dest = points // (n_lon * n_lat)
    capacity = ocean_current.shape[2]
    spectral = freqs * dirs
    tab = tables(freqs, dirs)
    everyone = ("lon", "lat")

    want = block_owner * capacity + block_slot
    ocean = lax.all_gather(ocean_current[:, 0], "lon", axis=1, tiled=True)
    sourced = source(tab, spec_pts, wind_u, wind_v)
    packed = sourced.reshape(spectral, points).T.reshape(n_lat, n_lon, per_dest, spectral)
    packed = packed.transpose(1, 0, 2, 3).reshape(n_lon * n_lat, per_dest, spectral)
    got = lax.all_to_all(packed, everyone, split_axis=0, concat_axis=0, tiled=True)
    recv = got.reshape(points, spectral)
    s, r = cell_source // per_dest, cell_source % per_dest
    cell = ((s % n_lon) * n_lat + s // n_lon) * per_dest + r
    tile, rows, cols, aux = regroup(recv, cell, land_mask, want, ocean)
    right = [(i, (i + 1) % n_lon) for i in range(n_lon)]
    left = [(j, i) for i, j in right]
    west = lax.ppermute(cols[1], "lon", right)
    east = lax.ppermute(cols[0], "lon", left)
    up = [(i, i + 1) for i in range(n_lat - 1)]
    down = [(j, i) for i, j in up]
    south = lax.ppermute(rows[1], "lat", up)
    north = lax.ppermute(rows[0], "lat", down)
    out = step(tab, tile, south, north, west, east, cols, aux)
    return out.reshape(freqs, dirs, lat_rows, lon_cells)


def solution(mesh):
    return jax.shard_map(
        body,
        mesh=mesh,
        in_specs=(
            P(None, None, ("lon", "lat")),
            P(("lon", "lat")),
            P(("lon", "lat")),
            P(None, "lat", "lon", None),
            P("lat", "lon"),
            P("lat", "lon"),
            P("lat", "lon"),
            P("lat", "lon"),
        ),
        out_specs=P(None, None, "lat", "lon"),
        check_vma=False,
    )
```

```python
import functools

import jax
import jax.numpy as jnp
import numpy as np
from jax import lax
from jax.experimental import pallas as pl
from jax.experimental.pallas import tpu as pltpu
from jax.sharding import PartitionSpec as P


fastest = 0.53
turn_scale = 2.5

GRANT = pltpu.CompilerParams(vmem_limit_bytes=20 * 1024 * 1024)
VMEM = pl.BlockSpec(memory_space=pltpu.VMEM)
SMEM = pl.BlockSpec(memory_space=pltpu.SMEM)


def tables(freqs, dirs):
    ratio = 1.1 ** np.arange(freqs)
    spacing = 2.0 * np.pi / dirs
    theta = (np.arange(dirs) + 0.5) * spacing
    facing = (np.arange(dirs) + 1.0) * spacing
    f32 = np.float32
    return dict(
        group=(fastest / ratio).astype(f32),
        slow=(ratio / 44.6).astype(f32),
        rel=(ratio / ratio[freqs - 1]).astype(f32),
        cosd=np.cos(theta).astype(f32),
        sind=np.sin(theta).astype(f32),
        fcos=np.cos(facing).astype(f32),
        fsin=np.sin(facing).astype(f32),
    )


def source_kernel(slow_ref, rel_ref, spec_ref, u_ref, v_ref, trig_ref, out_ref):
    freqs, dirs, points = spec_ref.shape

    def add(f, acc):
        return acc + spec_ref[f].astype(jnp.float32)

    acc = lax.fori_loop(0, freqs, add, jnp.zeros((dirs, points), jnp.float32), unroll=4)
    mean = jnp.sum(acc, axis=0, keepdims=True) / (freqs * dirs)
    base = 0.3 * (mean / 0.5) ** 2
    proj = u_ref[...] * trig_ref[:, 0:1] + v_ref[...] * trig_ref[:, 1:2]

    def one(f, carry):
        drive = jnp.maximum(proj * slow_ref[f] - 1.0, 0.0)
        gain = 0.5 * jnp.tanh(0.2 * drive)
        grown = spec_ref[f].astype(jnp.float32) * jnp.exp(gain - rel_ref[f] * base)
        out_ref[f] = grown.astype(jnp.bfloat16)
        return carry

    lax.fori_loop(0, freqs, one, 0, unroll=2)


def source(tab, spec, wind_u, wind_v):
    trig = np.stack([tab["cosd"], tab["sind"]], axis=1)
    return pl.pallas_call(
        source_kernel,
        out_shape=jax.ShapeDtypeStruct(spec.shape, jnp.bfloat16),
        in_specs=[SMEM, SMEM, VMEM, VMEM, VMEM, VMEM],
        out_specs=VMEM,
        name="source",
        compiler_params=GRANT,
    )(tab["slow"], tab["rel"], spec, wind_u[None], wind_v[None], trig)


def regroup_kernel(recv_ref, cell_ref, mask_ref, want_ref, ocean_ref, tile_ref, rows_ref, cols_ref, aux_ref):
    points, spectral = recv_ref.shape
    lat_rows, lon_cells = cell_ref.shape
    cell = cell_ref[...]
    mask = mask_ref[...]
    index = lax.broadcasted_iota(jnp.int32, (points, lon_cells), 0)
    hots = [
        jnp.where((index == cell[y : y + 1]) & (mask[y : y + 1] > 0), 1.0, 0.0).astype(jnp.bfloat16)
        for y in range(lat_rows)
    ]
    hot = jnp.concatenate(hots, axis=1)
    recv = recv_ref[...]
    dims = (((0,), (0,)), ((), ()))
    tile = lax.dot_general(recv, hot, dims, preferred_element_type=jnp.float32).astype(jnp.bfloat16)
    tile_ref[...] = tile
    blocks = ocean_ref.shape[1]
    pick = (lax.broadcasted_iota(jnp.int32, (lat_rows, blocks), 1) == want_ref[...]).astype(jnp.bfloat16)
    u = jnp.dot(pick, ocean_ref[0], preferred_element_type=jnp.float32)
    v = jnp.dot(pick, ocean_ref[1], preferred_element_type=jnp.float32)
    sea = mask.astype(jnp.float32)
    aux_ref[0] = u
    aux_ref[1] = v
    aux_ref[2] = sea
    for i, y in enumerate((0, lat_rows - 1)):
        rows_ref[i, :spectral] = tile[:, y * lon_cells : (y + 1) * lon_cells]
        extra = jnp.concatenate(
            [u[y : y + 1], v[y : y + 1], sea[y : y + 1], jnp.zeros((5, lon_cells), jnp.float32)], axis=0
        )
        rows_ref[i, spectral:] = extra.astype(jnp.bfloat16)
    lanes = lax.broadcasted_iota(jnp.int32, (lat_rows, points), 1)
    pad = cols_ref.shape[2] - spectral
    spot = lax.broadcasted_iota(jnp.int32, (lat_rows, pad), 1)
    for i, x in enumerate((0, lon_cells - 1)):
        edge = jnp.where((lanes == cell[:, x : x + 1]) & (mask[:, x : x + 1] > 0), 1.0, 0.0).astype(jnp.bfloat16)
        values = jnp.dot(edge, recv, preferred_element_type=jnp.float32)
        extra = jnp.where(
            spot == 0, u[:, x : x + 1], jnp.where(spot == 1, v[:, x : x + 1], jnp.where(spot == 2, sea[:, x : x + 1], 0.0))
        )
        cols_ref[i] = jnp.concatenate([values, extra], axis=1).astype(jnp.bfloat16)


def regroup(recv, cell, mask, want, ocean):
    points, spectral = recv.shape
    lat_rows, lon_cells = cell.shape
    wide = -(-(spectral + 3) // 128) * 128
    return pl.pallas_call(
        regroup_kernel,
        out_shape=(
            jax.ShapeDtypeStruct((spectral, points), jnp.bfloat16),
            jax.ShapeDtypeStruct((2, spectral + 8, lon_cells), jnp.bfloat16),
            jax.ShapeDtypeStruct((2, lat_rows, wide), jnp.bfloat16),
            jax.ShapeDtypeStruct((3, lat_rows, lon_cells), jnp.float32),
        ),
        in_specs=[VMEM] * 5,
        out_specs=(VMEM,) * 4,
        name="regroup",
        compiler_params=GRANT,
    )(recv, cell, mask, want, ocean)


def grow_four(four, spec_ref, slow_ref, rel_ref, proj, base, first):
    parts = []
    for q in range(4):
        f = first + 4 * four + q
        drive = jnp.maximum(proj * slow_ref[f] - 1.0, 0.0)
        gain = 0.5 * jnp.tanh(0.2 * drive)
        parts.append(spec_ref[f].astype(jnp.float32) * jnp.exp(gain - rel_ref[f] * base))
    return jnp.concatenate(parts, axis=0).astype(jnp.bfloat16)


def one_hot(index, depth):
    rows = lax.broadcasted_iota(jnp.int32, (depth, index.shape[1]), 0)
    return jnp.where(rows == index, 1.0, 0.0).astype(jnp.bfloat16)


class Route:
    def __init__(self, grid, n_lat, per):
        self.nz, self.nx, self.nc = grid
        self.ny, self.per = n_lat, per
        self.plane = self.nx * self.ny
        self.points = self.nz * self.nx * self.nc * n_lat * per

    def here(self):
        t = lax.axis_index("lon")
        return t // (self.nx * self.nc), t // self.nc % self.nx, t % self.nc, lax.axis_index("lat")

    def source_lane(self, z, x, c, y):
        n_lon = self.nz * self.nx * self.nc
        return (y * n_lon + (z * self.nx + x) * self.nc + c) * self.per

    def parts(self, sizes):
        q = lax.broadcasted_iota(jnp.int32, (1, self.points), 1)
        digits = []
        for n in (self.per, *reversed(sizes)):
            digits.append(q % n)
            q = q // n
        return digits[::-1]

    def b1(self):
        z, _, _, _ = self.here()
        gz, yd, xd, cd, r = self.parts((self.nz, self.ny, self.nx, self.nc))
        return self.source_lane((z + gz) % self.nz, xd, cd, yd) + r

    def b2(self):
        _, x, _, y = self.here()
        gx, gy, gz, cd, r = self.parts((self.nx, self.ny, self.nz, self.nc))
        xd, yd = (x + gx) % self.nx, (y + gy) % self.ny
        return (((gz * self.ny + yd) * self.nx + xd) * self.nc + cd) * self.per + r

    def b3(self):
        _, _, c, _ = self.here()
        gc, g, gz, r = self.parts((self.nc, self.plane, self.nz))
        return ((g * self.nz + gz) * self.nc + (c + gc) % self.nc) * self.per + r

    def a1(self):
        _, _, c, _ = self.here()
        gc, yd, zd, xd, r = self.parts((self.nc, self.ny, self.nz, self.nx))
        return self.source_lane(zd, xd, (c + gc) % self.nc, yd) + r

    def a2(self):
        _, x, _, y = self.here()
        gx, gy, gc, zd, r = self.parts((self.nx, self.ny, self.nc, self.nz))
        xd, yd = (x + gx) % self.nx, (y + gy) % self.ny
        return (((gc * self.ny + yd) * self.nz + zd) * self.nx + xd) * self.per + r

    def a3(self):
        z, _, _, _ = self.here()
        gz, g, gc, r = self.parts((self.nz, self.plane, self.nc))
        return ((g * self.nc + gc) * self.nz + (z + gz) % self.nz) * self.per + r

    def split(self, cell):
        z, x, c, y = self.here()
        n_lon = self.nz * self.nx * self.nc
        r, s = cell % self.per, cell // self.per
        a, b = s % n_lon, s // n_lon
        za, xa, ca = a // (self.nx * self.nc), a // self.nc % self.nx, a % self.nc
        gz, gx = (z - za + self.nz) % self.nz, (x - xa + self.nx) % self.nx
        gc, gy = (c - ca + self.nc) % self.nc, (y - b + self.ny) % self.ny
        return gz, gx, gc, gy, r

    def b_end(self, cell):
        gz, gx, gc, gy, r = self.split(cell)
        return ((gc * self.plane + gx * self.ny + gy) * self.nz + gz) * self.per + r

    def a_end(self, cell):
        gz, gx, gc, gy, r = self.split(cell)
        return ((gz * self.plane + gx * self.ny + gy) * self.nc + gc) * self.per + r

    def shift(self, axis_steps):
        dz, dx, dc, dy = axis_steps
        pairs = []
        for z in range(self.nz):
            for x in range(self.nx):
                for c in range(self.nc):
                    for y in range(self.ny):
                        a = ((z + dz) % self.nz * self.nx + (x + dx) % self.nx) * self.nc + (c + dc) % self.nc
                        here = ((z * self.nx + x) * self.nc + c) * self.ny + y
                        pairs.append((here, a * self.ny + (y + dy) % self.ny))
        return pairs


def source_b_kernel(route, first, slow_ref, rel_ref, spec_ref, u_ref, v_ref, trig_ref, ocean_ref, *rest):
    *out_refs, base_ref, hot = rest
    freqs, dirs, points = spec_ref.shape
    hot[...] = one_hot(route.b1(), points)

    def add(f, acc):
        return acc + spec_ref[f].astype(jnp.float32)

    acc = lax.fori_loop(0, freqs, add, jnp.zeros((dirs, points), jnp.float32), unroll=4)
    mean = jnp.sum(acc, axis=0, keepdims=True) / (freqs * dirs)
    base = 0.3 * (mean / 0.5) ** 2
    base_ref[...] = base
    proj = u_ref[...] * trig_ref[:, 0:1] + v_ref[...] * trig_ref[:, 1:2]
    size = 4 * dirs
    rows, lanes = out_refs[0].shape

    def four(i, carry):
        grown = grow_four(i, spec_ref, slow_ref, rel_ref, proj, base, first)
        moved = jnp.dot(grown, hot[...], preferred_element_type=jnp.float32).astype(jnp.bfloat16)
        at = pl.ds(pl.multiple_of(i * size, 16), size)
        for g, out in enumerate(out_refs):
            out[at] = moved[:, g * lanes : (g + 1) * lanes]
        return carry

    lax.fori_loop(0, rows // size, four, 0)
    for out in out_refs[1:]:
        out[rows:] = ocean_ref[...]


def source_a_kernel(route, first, slow_ref, rel_ref, spec_ref, u_ref, v_ref, trig_ref, base_ref, *rest):
    *out_refs, hot = rest
    _, dirs, points = spec_ref.shape
    hot[...] = one_hot(route.a1(), points)
    proj = u_ref[...] * trig_ref[:, 0:1] + v_ref[...] * trig_ref[:, 1:2]
    base = base_ref[...]
    size = 4 * dirs
    rows, lanes = out_refs[0].shape

    def four(i, carry):
        grown = grow_four(i, spec_ref, slow_ref, rel_ref, proj, base, first)
        moved = jnp.dot(grown, hot[...], preferred_element_type=jnp.float32).astype(jnp.bfloat16)
        at = pl.ds(pl.multiple_of(i * size, 16), size)
        for g, out in enumerate(out_refs):
            out[at] = moved[:, g * lanes : (g + 1) * lanes]
        return carry

    lax.fori_loop(0, rows // size, four, 0)


def bf16(*shape):
    return jax.ShapeDtypeStruct(shape, jnp.bfloat16)


def hot_scratch(points):
    return [pltpu.VMEM((points, points), jnp.bfloat16)]


def source_b(tab, route, first, count, spec, wind_u, wind_v, ocean):
    _, dirs, points = spec.shape
    trig = np.stack([tab["cosd"], tab["sind"]], axis=1)
    k, lanes = count * dirs, points // route.nz
    more = ocean.shape[0]
    outs = [bf16(k, lanes)] + [bf16(k + more, lanes)] * (route.nz - 1)

    def kernel(slow, rel, spec_ref, u, v, trig_ref, ocean_ref, *rest):
        outs_ = rest[: route.nz]
        own, sent = outs_[0], outs_[1:]
        source_b_kernel(route, first, slow, rel, spec_ref, u, v, trig_ref, ocean_ref, own, *sent, *rest[route.nz :])

    return pl.pallas_call(
        kernel,
        out_shape=(*outs, jax.ShapeDtypeStruct((1, points), jnp.float32)),
        in_specs=[SMEM, SMEM] + [VMEM] * 5,
        out_specs=(VMEM,) * (route.nz + 1),
        scratch_shapes=hot_scratch(points),
        name="source_b",
        compiler_params=GRANT,
    )(tab["slow"], tab["rel"], spec, wind_u[None], wind_v[None], trig, ocean)


def source_a(tab, route, first, count, spec, wind_u, wind_v, base):
    _, dirs, points = spec.shape
    trig = np.stack([tab["cosd"], tab["sind"]], axis=1)
    return pl.pallas_call(
        functools.partial(source_a_kernel, route, first),
        out_shape=(bf16(count * dirs, points // route.nc),) * route.nc,
        in_specs=[SMEM, SMEM] + [VMEM] * 5,
        out_specs=(VMEM,) * route.nc,
        scratch_shapes=hot_scratch(points),
        name="source_a",
        compiler_params=GRANT,
    )(tab["slow"], tab["rel"], spec, wind_u[None], wind_v[None], trig, base)


def shuffle(index, size, ins, outs, points, n_in, n_out, extra=None):
    return pl.pallas_call(
        functools.partial(shuffle_body, index, size, n_in, len(ins), n_out, extra),
        out_shape=tuple(outs),
        in_specs=[VMEM] * len(ins),
        out_specs=(VMEM,) * len(outs),
        scratch_shapes=hot_scratch(points),
        compiler_params=GRANT,
    )(*ins)


def shuffle_body(index, size, n_in, n_all, n_out, extra, *refs):
    ins, hot = refs[:n_in], refs[-1]
    others, outs = refs[n_in:n_all], refs[n_all:-1]
    hot[...] = one_hot(index(), hot.shape[0])
    rows = ins[0].shape[0]
    lanes = outs[0].shape[1]

    def block(i, carry):
        at = pl.ds(pl.multiple_of(i * size, 16), size)
        have = jnp.concatenate([r[at] for r in ins], axis=1)
        moved = jnp.dot(have, hot[...], preferred_element_type=jnp.float32).astype(jnp.bfloat16)
        for g in range(n_out):
            outs[g][at] = moved[:, g * lanes : (g + 1) * lanes]
        return carry

    lax.fori_loop(0, rows // size, block, 0)
    if extra:
        extra(rows, ins, others, outs)


def swap(parts, perms):
    moved = []
    for part, perm in zip(parts, perms):
        moved.append(lax.ppermute(part, ("lon", "lat"), perm))
    return moved


def exchange_b(route, size, parts, ocean):
    points, k = route.points, parts[0].shape[0]
    nz, nx, ny, nc = route.nz, route.nx, route.ny, route.nc
    more = ocean.shape[0]
    lanes = points // nz
    got = swap(parts[1:], [route.shift((d, 0, 0, 0)) for d in range(1, nz)])
    steps = [(gx, gy) for gx in range(nx) for gy in range(ny)]
    column = [i for i, (gx, gy) in enumerate(steps) if gy == 0]

    def gather_z(rows, ins, others, outs):
        blocks = [others[0][...]] + [r[rows:] for r in ins[1:]]
        whole = jnp.concatenate(blocks, axis=0)
        outs[-1][...] = whole
        for i in column[1:]:
            outs[i][rows:] = whole

    wide = points // len(steps)
    outs = [bf16(k + (nz * more if i in column[1:] else 0), wide) for i in range(len(steps))]
    *parts, ocean_z = shuffle(
        route.b2, size, [parts[0], *got, ocean], [*outs, bf16(nz * more, lanes)], points, nz, len(steps), gather_z
    )
    got = swap(parts[1:], [route.shift((0, gx, 0, gy)) for gx, gy in steps[1:]])

    def gather_x(rows, ins, others, outs):
        blocks = [others[0][...]] + [ins[i][rows:] for i in column[1:]]
        whole = jnp.concatenate(blocks, axis=1)
        outs[-1][...] = whole
        for out in outs[1:nc]:
            out[rows:] = whole

    deep, side = nz * more, nx * lanes
    outs = [bf16(k, points // nc)] + [bf16(k + deep, points // nc)] * (nc - 1) + [bf16(deep, side)]
    keep, *sent, ocean_x = shuffle(route.b3, size, [parts[0], *got, ocean_z], outs, points, len(steps), nc, gather_x)
    got = swap(sent, [route.shift((0, 0, d, 0)) for d in range(1, nc)])
    return [keep, *got], ocean_x


def exchange_a(route, size, parts):
    points, k = route.points, parts[0].shape[0]
    nz, nx, ny, nc = route.nz, route.nx, route.ny, route.nc
    got = swap(parts[1:], [route.shift((0, 0, d, 0)) for d in range(1, nc)])
    steps = [(gx, gy) for gx in range(nx) for gy in range(ny)]
    outs = [bf16(k, points // len(steps))] * len(steps)
    parts = shuffle(route.a2, size, [parts[0], *got], outs, points, nc, len(steps))
    got = swap(parts[1:], [route.shift((0, gx, 0, gy)) for gx, gy in steps[1:]])
    parts = shuffle(route.a3, size, [parts[0], *got], [bf16(k, points // nz)] * nz, points, len(steps), nz)
    got = swap(parts[1:], [route.shift((d, 0, 0, 0)) for d in range(1, nz)])
    return [parts[0], *got]


def tile_of(size, parts, hot, tile_ref):
    def block(i, carry):
        at = pl.ds(pl.multiple_of(i * size, 16), size)
        have = jnp.concatenate([r[at] for r in parts], axis=1)
        tile_ref[at] = jnp.dot(have, hot[...], preferred_element_type=jnp.float32).astype(jnp.bfloat16)
        return carry

    lax.fori_loop(0, tile_ref.shape[0] // size, block, 0)


def cells_hot(place, mask, hot):
    lat_rows, lon_cells = mask.shape
    index = lax.broadcasted_iota(jnp.int32, (hot.shape[0], lon_cells), 0)
    for y in range(lat_rows):
        chosen = (index == place[y : y + 1]) & (mask[y : y + 1] > 0)
        hot[:, y * lon_cells : (y + 1) * lon_cells] = jnp.where(chosen, 1.0, 0.0).astype(jnp.bfloat16)


def regroup_b_kernel(route, size, n_parts, capacity, *refs):
    parts = refs[:n_parts]
    ocean_ref, owner_ref, slot_ref, cell_ref, mask_ref, tile_ref, aux_ref, hot = refs[n_parts:]
    mask = mask_ref[...]
    cells_hot(route.b_end(cell_ref[...]), mask, hot)
    k = tile_ref.shape[0]
    tile_of(size, parts, hot, tile_ref)
    lat_rows, lon_cells = mask.shape
    owner = owner_ref[...]
    z, x, c, _ = route.here()
    za, xa, ca = owner // (route.nx * route.nc), owner // route.nc % route.nx, owner % route.nc
    gz, gx = (z - za + route.nz) % route.nz, (x - xa + route.nx) % route.nx
    gc = (c - ca + route.nc) % route.nc
    deep = ocean_ref.shape[0]
    spot = lax.broadcasted_iota(jnp.int32, (lat_rows, deep), 1)
    at = gz * (2 * capacity) + slot_ref[...]
    u = v = 0.0
    for i in range(route.nc):
        for j in range(route.nx):
            lanes = slice(j * lon_cells, (j + 1) * lon_cells)
            block = ocean_ref[:, lanes] if i == 0 else parts[i][k:, lanes]
            here = (gc == i) & (gx == j)
            u += jnp.dot(jnp.where((spot == at) & here, 1.0, 0.0).astype(jnp.bfloat16), block, preferred_element_type=jnp.float32)
            v += jnp.dot(
                jnp.where((spot == at + capacity) & here, 1.0, 0.0).astype(jnp.bfloat16), block, preferred_element_type=jnp.float32
            )
    aux_ref[0] = u
    aux_ref[1] = v
    aux_ref[2] = mask.astype(jnp.float32)


def regroup_b(route, size, parts, ocean, owner, slot, cell, mask, capacity):
    lat_rows, lon_cells = cell.shape
    return pl.pallas_call(
        functools.partial(regroup_b_kernel, route, size, len(parts), capacity),
        out_shape=(bf16(parts[0].shape[0], route.points), jax.ShapeDtypeStruct((3, lat_rows, lon_cells), jnp.float32)),
        in_specs=[VMEM] * (len(parts) + 5),
        out_specs=(VMEM,) * 2,
        scratch_shapes=hot_scratch(route.points),
        name="regroup_b",
        compiler_params=GRANT,
    )(*parts, ocean, owner, slot, cell, mask)


def pick_column(y_cells, x, lat_rows, lon_cells):
    want = lax.broadcasted_iota(jnp.int32, (lat_rows, y_cells), 0) * lon_cells + x
    return jnp.where(lax.broadcasted_iota(jnp.int32, (lat_rows, y_cells), 1) == want, 1.0, 0.0).astype(jnp.bfloat16)


def regroup_a_kernel(route, size, n_parts, *refs):
    parts = refs[:n_parts]
    cell_ref, mask_ref, first_ref, aux_ref, tile_ref, row_ref, near_ref, far_ref, west_ref, hot = refs[n_parts:]
    mask = mask_ref[...]
    lat_rows, lon_cells = mask.shape
    points = route.points
    cells_hot(route.a_end(cell_ref[...]), mask, hot)
    tile_of(size, parts, hot, tile_ref)
    kb, ka = first_ref.shape[0], tile_ref.shape[0]
    spectral = kb + ka
    u, v, sea = aux_ref[0], aux_ref[1], aux_ref[2]
    _, _, c, y = route.here()
    facing = y == 0
    last = (lat_rows - 1) * lon_cells
    row_ref[:kb] = jnp.where(facing, first_ref[:, last : last + lon_cells], first_ref[:, :lon_cells])
    row_ref[kb:spectral] = jnp.where(facing, tile_ref[:, last : last + lon_cells], tile_ref[:, :lon_cells])
    low = jnp.concatenate([u[:1], v[:1], sea[:1], jnp.zeros((5, lon_cells), jnp.float32)], axis=0)
    high = jnp.concatenate([u[-1:], v[-1:], sea[-1:], jnp.zeros((5, lon_cells), jnp.float32)], axis=0)
    row_ref[spectral:] = jnp.where(facing, high, low).astype(jnp.bfloat16)
    contract = (((1,), (1,)), ((), ()))
    pad = near_ref.shape[1] - spectral
    spot = lax.broadcasted_iota(jnp.int32, (lat_rows, pad), 1)
    cols = []
    for at in (0, lon_cells - 1):
        pick = pick_column(points, at, lat_rows, lon_cells)
        one = lax.dot_general(pick, first_ref[...], contract, preferred_element_type=jnp.float32)
        two = lax.dot_general(pick, tile_ref[...], contract, preferred_element_type=jnp.float32)
        extra = jnp.where(
            spot == 0, u[:, at : at + 1], jnp.where(spot == 1, v[:, at : at + 1], jnp.where(spot == 2, sea[:, at : at + 1], 0.0))
        )
        cols.append(jnp.concatenate([one, two, extra], axis=1))
    west, east = cols
    near_ref[...] = jnp.where(c % 2 == 0, east, west).astype(jnp.bfloat16)
    far_ref[...] = jnp.where(c % 2 == 0, west, east).astype(jnp.bfloat16)
    west_ref[...] = west.astype(jnp.bfloat16)


def regroup_a(route, size, parts, cell, mask, first, aux):
    lat_rows, lon_cells = cell.shape
    k = parts[0].shape[0]
    spectral = k + first.shape[0]
    wide = -(-(spectral + 3) // 128) * 128
    edge = bf16(lat_rows, wide)
    return pl.pallas_call(
        functools.partial(regroup_a_kernel, route, size, len(parts)),
        out_shape=(bf16(k, route.points), bf16(spectral + 8, lon_cells), edge, edge, edge),
        in_specs=[VMEM] * (len(parts) + 4),
        out_specs=(VMEM,) * 5,
        scratch_shapes=hot_scratch(route.points),
        name="regroup_a",
        compiler_params=GRANT,
    )(*parts, cell, mask, first, aux)


def upwind(speed, here, there):
    return jnp.where(speed > 0.0, here, there) * speed


def step_kernel(route, n_tiles, group_ref, *refs):
    tiles = refs[:n_tiles]
    south_ref, north_ref, west_ref, east_ref, own_ref, aux_ref, trig_ref, freq_ref, out_ref, halo, turns, lay = refs[n_tiles:]
    spectral = sum(t.shape[0] for t in tiles)
    rows, lanes = turns.shape[1], aux_ref.shape[2]
    lat_rows = aux_ref.shape[1]
    dirs = rows // 2
    f32 = jnp.float32
    u, v, sea = aux_ref[0], aux_ref[1], aux_ref[2]
    lane = lax.broadcasted_iota(jnp.int32, (lat_rows, lanes), 1)
    below = south_ref[spectral : spectral + 8].astype(f32)
    above = north_ref[spectral : spectral + 8].astype(f32)
    west_b, east_b = west_ref[...], east_ref[...]
    if route:
        _, _, c, y = route.here()
        below = jnp.where(y == 1, below, 0.0)
        above = jnp.where(y == 0, above, 0.0)
        west_b, east_b = jnp.where(c % 2 == 0, east_b, west_b), jnp.where(c % 2 == 0, west_b, east_b)
    west, east = west_b.astype(f32), east_b.astype(f32)

    def sides(a, i):
        at = spectral + i
        right = jnp.where(lane == lanes - 1, east[:, at : at + 1], pltpu.roll(a, lanes - 1, 1))
        left = jnp.where(lane == 0, west[:, at : at + 1], pltpu.roll(a, 1, 1))
        return left, right

    uw, ue = sides(u, 0)
    vw, ve = sides(v, 1)
    _, me = sides(sea, 2)
    open_x = sea * me
    face_u = 0.5 * (u + ue)
    ut = jnp.concatenate([below[0:1], u, above[0:1]], axis=0)
    vt = jnp.concatenate([below[1:2], v, above[1:2]], axis=0)
    mt = jnp.concatenate([below[2:3], sea, above[2:3]], axis=0)
    open_y = mt[:-1] * mt[1:]
    face_v = 0.5 * (vt[:-1] + vt[1:])
    ux = 0.5 * (ue - uw)
    vx = 0.5 * (ve - vw)
    uy = 0.5 * (ut[2:] - ut[:-2])
    vy = 0.5 * (vt[2:] - vt[:-2])
    fc, fs = trig_ref[:, 2:3], trig_ref[:, 3:4]
    for y in range(lat_rows):
        sl = slice(y, y + 1)
        turns[y] = turn_scale * (fs * fc * (ux[sl] - vy[sl]) + fs * fs * uy[sl] - fc * fc * vx[sl])
    own = own_ref[:, :spectral].astype(f32)
    wide_u = west[:, spectral : spectral + 1]
    speed = freq_ref[0:1] + 0.5 * (wide_u + u[:, 0:1])
    flux_w = (west[:, spectral + 2 : spectral + 3] * sea[:, 0:1]) * upwind(speed, west[:, :spectral], own)
    hi = flux_w.astype(jnp.bfloat16)
    rest = flux_w - hi.astype(f32)
    mid = rest.astype(jnp.bfloat16)
    low = (rest - mid.astype(f32)).astype(jnp.bfloat16)
    left = jnp.concatenate([hi, mid, low, east_b[:, :spectral]], axis=0)
    total = lat_rows * lanes
    j = lax.broadcasted_iota(jnp.int32, (4 * lat_rows, total), 0)
    c = lax.broadcasted_iota(jnp.int32, (4 * lat_rows, total), 1)
    part, jy = j // lat_rows, j % lat_rows
    place = jnp.where(c == jy * lanes + jnp.where(part == 3, lanes - 1, 0), 1.0, 0.0).astype(jnp.bfloat16)
    halo[...] = lax.dot_general(left, place, (((0,), (0,)), ((), ())), preferred_element_type=f32)

    row = lax.broadcasted_iota(jnp.int32, (rows, lanes), 0)
    full_lane = lax.broadcasted_iota(jnp.int32, (rows, lanes), 1)
    is_last, is_first = full_lane == lanes - 1, full_lane == 0
    top = row < dirs
    seam_up = (row == dirs - 1) | (row == rows - 1)
    seam_down = (row == 0) | (row == dirs)
    cosd, sind = trig_ref[:, 0:1], trig_ref[:, 1:2]

    def pair(tile_ref, start, i, carry):
        mine = pl.ds(pl.multiple_of(i * rows, 8), rows)
        at = pl.multiple_of(start + i * rows, 8)
        sl = pl.ds(at, rows)
        f = start // dirs + 2 * i
        speed_f = jnp.where(top, group_ref[f], group_ref[f + 1])
        gc = speed_f * cosd
        gs = speed_f * sind
        value = [tile_ref[mine, y * lanes : (y + 1) * lanes].astype(f32) for y in range(lat_rows)]
        below_v = south_ref[sl, :].astype(f32)
        above_v = north_ref[sl, :].astype(f32)
        flux_s = None
        for y in range(lat_rows + 1):
            lower = below_v if y == 0 else value[y - 1]
            upper = above_v if y == lat_rows else value[y]
            cy = gs + face_v[y : y + 1]
            flux_n = open_y[y : y + 1] * upwind(cy, lower, upper)
            if y > 0:
                k = y - 1
                e = value[k]
                edge = halo[sl, k * lanes : (k + 1) * lanes]
                ee = jnp.where(is_last, edge, pltpu.roll(e, lanes - 1, 1))
                cx = gc + face_u[k : k + 1]
                fx = open_x[k : k + 1] * upwind(cx, e, ee)
                fw = jnp.where(is_first, edge, pltpu.roll(fx, 1, 1))
                moved = e - (fx - fw) - (flux_n - flux_s)
                up = jnp.where(seam_up, pltpu.roll(moved, dirs - 1, 0), pltpu.roll(moved, rows - 1, 0))
                g = upwind(turns[k], moved, up)
                gp = jnp.where(seam_down, pltpu.roll(g, dirs + 1, 0), pltpu.roll(g, 1, 0))
                lay[pl.ds(k, rows, stride=lat_rows), :] = (moved - (g - gp)) * sea[k : k + 1]
            flux_s = flux_n
        out_ref[pl.ds(pl.multiple_of(at * lat_rows, 8), rows * lat_rows), :] = lay[...].astype(jnp.bfloat16)
        return carry

    start = 0
    for t in tiles:
        lax.fori_loop(0, t.shape[0] // rows, functools.partial(pair, t, start), 0)
        start += t.shape[0]


def step(tab, route, tiles, south, north, west, east, own, aux):
    freqs, dirs = tab["group"].shape[0], tab["cosd"].shape[0]
    spectral, points = freqs * dirs, tiles[0].shape[1]
    _, lat_rows, lon_cells = aux.shape
    trig = np.tile(np.stack([tab["cosd"], tab["sind"], tab["fcos"], tab["fsin"]], axis=1), (2, 1))
    freq = np.outer(tab["group"], tab["cosd"]).reshape(1, spectral)
    return pl.pallas_call(
        functools.partial(step_kernel, route, len(tiles)),
        out_shape=jax.ShapeDtypeStruct((spectral * lat_rows, lon_cells), jnp.bfloat16),
        in_specs=[SMEM] + [VMEM] * (len(tiles) + 8),
        out_specs=VMEM,
        scratch_shapes=[
            pltpu.VMEM((spectral, points), jnp.float32),
            pltpu.VMEM((lat_rows, 2 * dirs, lon_cells), jnp.float32),
            pltpu.VMEM((2 * dirs * lat_rows, lon_cells), jnp.float32),
        ],
        name="step",
        compiler_params=GRANT,
    )(tab["group"], *tiles, south, north, west, east, own, aux, trig, freq)


def lon_grid(mesh):
    spots = [(d.coords[2], d.coords[0], d.core_on_chip) for d in mesh.devices[:, 0] if hasattr(d, "coords")]
    if len(spots) != mesh.shape["lon"]:
        return None
    sizes = tuple(len({s[i] for s in spots}) for i in range(3))
    base = [min(s[i] for s in spots) for i in range(3)]
    flat = [((s[0] - base[0]) * sizes[1] + s[1] - base[1]) * sizes[2] + s[2] - base[2] for s in spots]
    return sizes if flat == list(range(len(spots))) else None


def body(grid, spec_pts, wind_u, wind_v, ocean_current, block_owner, block_slot, cell_source, land_mask):
    freqs, dirs, points = spec_pts.shape
    lat_rows, lon_cells = cell_source.shape
    n_lon, n_lat = lax.axis_size("lon"), lax.axis_size("lat")
    per_dest = points // (n_lon * n_lat)
    capacity = ocean_current.shape[2]
    spectral = freqs * dirs
    tab = tables(freqs, dirs)
    if staged(grid, n_lat):
        route = Route(grid, n_lat, per_dest)
        count = -(-freqs * 5 // 9) // 4 * 4
        size = 4 * dirs
        ocean = ocean_current.reshape(2 * capacity, lon_cells)
        *parts, base = source_b(tab, route, 0, count, spec_pts, wind_u, wind_v, ocean)
        parts_a = source_a(tab, route, count, freqs - count, spec_pts, wind_u, wind_v, base)
        parts, ocean = exchange_b(route, size, parts, ocean)
        parts_a = exchange_a(route, size, parts_a)
        tile_b, aux = regroup_b(route, size, parts, ocean, block_owner, block_slot, cell_source, land_mask, capacity)
        tile_a, row, near, far, own = regroup_a(route, size, parts_a, cell_source, land_mask, tile_b, aux)
        ring = [(i, (i - 1) % n_lon if i % 2 == 0 else (i + 1) % n_lon) for i in range(n_lon)]
        chip = [(i, i ^ 1) for i in range(n_lon)]
        row = lax.ppermute(row, "lat", [(0, 1), (1, 0)])
        far = lax.ppermute(far, "lon", ring)
        near = lax.ppermute(near, "lon", chip)
        out = step(tab, route, [tile_b, tile_a], row, row, near, far, own, aux)
        return out.reshape(freqs, dirs, lat_rows, lon_cells)
    everyone = ("lon", "lat")
    want = block_owner * capacity + block_slot
    ocean = lax.all_gather(ocean_current[:, 0], "lon", axis=1, tiled=True)
    sourced = source(tab, spec_pts, wind_u, wind_v)
    packed = sourced.reshape(spectral, points).T.reshape(n_lat, n_lon, per_dest, spectral)
    packed = packed.transpose(1, 0, 2, 3).reshape(n_lon * n_lat, per_dest, spectral)
    got = lax.all_to_all(packed, everyone, split_axis=0, concat_axis=0, tiled=True)
    recv = got.reshape(points, spectral)
    s, r = cell_source // per_dest, cell_source % per_dest
    cell = ((s % n_lon) * n_lat + s // n_lon) * per_dest + r
    tile, rows, cols, aux = regroup(recv, cell, land_mask, want, ocean)
    right = [(i, (i + 1) % n_lon) for i in range(n_lon)]
    left = [(j, i) for i, j in right]
    west = lax.ppermute(cols[1], "lon", right)
    east = lax.ppermute(cols[0], "lon", left)
    up = [(i, i + 1) for i in range(n_lat - 1)]
    down = [(j, i) for i, j in up]
    south = lax.ppermute(rows[1], "lat", up)
    north = lax.ppermute(rows[0], "lat", down)
    out = step(tab, None, [tile], south, north, west, east, cols[0], aux)
    return out.reshape(freqs, dirs, lat_rows, lon_cells)


def staged(grid, n_lat):
    return bool(grid) and n_lat == 2 and grid[2] == 2


def solution(mesh):
    grid = lon_grid(mesh)

    def layer(*args):
        return body(grid, *args)

    return jax.shard_map(
        layer,
        mesh=mesh,
        in_specs=(
            P(None, None, ("lon", "lat")),
            P(("lon", "lat")),
            P(("lon", "lat")),
            P(None, "lat", "lon", None),
            P("lat", "lon"),
            P("lat", "lon"),
            P("lat", "lon"),
            P("lat", "lon"),
        ),
        out_specs=P(None, None, "lat", "lon"),
        check_vma=False,
    )
```
